32 devices in a mesh: grp: 2 (over y), prow: 4 (over z), pcol: 4 (over x, core).
Axes of the slice: x: 2, y: 2, z: 4, core: 2. Of those that a mesh axis runs over, the one named last changes fastest.
Arguments:
- eigvecs: float32 [8192, 4096], P(('grp', 'prow'), 'pcol'), parts along dimension 0, may hold values from -6 to 6
- y_panels: float32 [2, 8192, 256], P(None, ('grp', 'prow'), 'pcol'), parts along dimension 1, as said below
- t_factors: float32 [4, 256, 256], P('grp'), parts along dimension 0, as said below
Outputs:
- result: float32 [8192, 4096], P(('grp', 'prow'), 'pcol'), parts along dimension 0
The draws below stay inside these ranges and needn't reach their ends.
There are 2 independent parts, one for each index of `grp`. The reference program is written for one: setup_inputs(seed, part) draws one part's arguments, and reference() takes and returns one part's arrays. A program takes and returns all parts, laid end to end along the dimension named above; each array names one. Nothing has to cross between parts.
Inputs may be any that keep to these rules, and one draw needn't show every extreme that they name: `y_panels`: column j of panel k is zero in rows above k * 256 + j and one in that row; t_factors[k] is upper triangular with diagonal between 0.5 and 1.5. Each t_factors[k] is upper triangular.
All inputs are finite; a program needn't handle non-finite values.
Results may differ from the reference program's by a relative error of at most 0.0001.
Values sent between devices are 32-bit elements; how exact they have to be, the bound alone decides.
No kernel may reach another device: no remote copies, remote signals or barrier semaphores. Data moves between devices by JAX's collectives and lax.ppermute only.
A program may use at most 64 MiB of HBM per device.

```python
import jax
import jax.numpy as jnp
from jax import lax

NB = 256
PANELS = 2
NCOLS = 4096
SUPPORT = 4096


def draw_y_panels(key, part):
    inner = jax.random.fold_in(key, 11)
    raw = jax.random.truncated_normal(inner, -4.0, 4.0, (PANELS, SUPPORT, NB), jnp.float32)
    raw = raw / jnp.sqrt(jnp.float32(SUPPORT))
    rowidx = jnp.arange(SUPPORT, dtype=jnp.int32)[None, :, None]
    colidx = jnp.arange(NB, dtype=jnp.int32)[None, None, :]
    panel = jnp.arange(PANELS, dtype=jnp.int32)[:, None, None]
    diagrow = panel * NB + colidx
    ones = jnp.where(rowidx == diagrow, 1.0, 0.0).astype(jnp.float32)
    return jnp.where(rowidx > diagrow, raw, ones).astype(jnp.float32)


def draw_t_factors(key, part):
    first = jax.random.fold_in(key, 21)
    second = jax.random.fold_in(key, 22)
    logs = jax.random.uniform(first, (PANELS, NB), jnp.float32, jnp.log(0.5), jnp.log(1.5))
    upper = jax.random.truncated_normal(second, -4.0, 4.0, (PANELS, NB, NB), jnp.float32)
    upper = upper * 0.5 / jnp.sqrt(jnp.float32(NB))
    rowidx = jnp.arange(NB, dtype=jnp.int32)[:, None]
    colidx = jnp.arange(NB, dtype=jnp.int32)[None, :]
    strict = jnp.where(colidx > rowidx, upper, 0.0)
    diagonal = jnp.exp(logs)[:, :, None] * jnp.where(colidx == rowidx, 1.0, 0.0)[None]
    return (strict + diagonal).astype(jnp.float32)


def level_of(rng, dims, split, least, high):
    def one(position, parts):
        draws = jax.random.uniform(jax.random.fold_in(jax.random.fold_in(rng, 6), position), (parts,), jnp.float32, least / len(split), high / len(split))
        return jnp.repeat(jnp.exp(draws), dims[position] // parts).reshape((-1,) + (1,) * (len(dims) - position - 1))

    factor_of = one(*split[0])
    for cut in split[1:]:
        factor_of = factor_of * one(*cut)
    return factor_of


def noise(rng, shape, spread, bound, split=(), kind=jnp.bfloat16):
    loudness = level_of(rng, shape, split, -0.22, 0.18) if split else 1.0
    result = jax.random.normal(rng, shape, jnp.float32) * spread * loudness
    return jnp.minimum(jnp.maximum(result, -bound), bound).astype(kind)


def setup_inputs(seed: int = 0, part: int = 0) -> dict:
    key_list = jax.random.split(jax.random.key(seed), 4)
    part_splits = jax.random.split(jax.random.fold_in(key_list[3], part), 4)
    eigvecs = noise(part_splits[0], (SUPPORT, NCOLS), 1.0, 6.0, ((0, 4), (1, 4)), jnp.float32)
    y_panels = draw_y_panels(jax.random.fold_in(jax.random.fold_in(key_list[3], part), 71), part)
    t_factors = draw_t_factors(jax.random.fold_in(jax.random.fold_in(key_list[3], part), 71), part)
    return {"eigvecs": eigvecs, "y_panels": y_panels, "t_factors": t_factors}


def reference(eigvecs, y_panels, t_factors):
    highest = lax.Precision.HIGHEST
    current = eigvecs
    for index in reversed(range(PANELS)):
        vectors = y_panels[index]
        sums = jnp.einsum("rc,rk->ck", current, vectors, precision=highest)
        scaled = jnp.einsum("ck,jk->cj", sums, t_factors[index], precision=highest)
        current = current - jnp.einsum("rj,cj->rc", vectors, scaled, precision=highest)
    return current
```

```python
import jax
import jax.numpy as jnp
from jax import lax
from jax.sharding import PartitionSpec as P

LAG_M = 2
LAG_E = 4
SPLIT = 4
HIGH = lax.Precision.HIGH
CORE = ((0, 1), (1, 0), (2, 3), (3, 2))
ACROSS = ((0, 2), (2, 0), (1, 3), (3, 1))
EDGE = ((0, 1), (1, 0), (2, 3), (3, 2))
MIDDLE = ((1, 2), (2, 1))


def update(current, vectors, triangle):
    highest = lax.Precision.HIGHEST
    local_sums = jnp.einsum("rc,rk->ck", current, vectors, precision=highest)
    sums = lax.psum(local_sums, "prow")
    scaled = jnp.einsum("ck,jk->cj", sums, triangle, precision=highest)
    return current - jnp.einsum("rj,cj->rc", vectors, scaled, precision=highest)


def ring_form(eigvecs, y_panels, t_factors):
    gathered = lax.all_gather(y_panels, "pcol", axis=2, tiled=True)
    current = eigvecs
    for index in reversed(range(gathered.shape[0])):
        current = update(current, gathered[index], t_factors[index])
    return current


def mm(a, b, ca, cb):
    return lax.dot_general(
        a, b, (((ca,), (cb,)), ((), ())), precision=HIGH, preferred_element_type=jnp.float32
    )


def relative_blocks(t, place):
    n, size, _ = t.shape
    b = size // 4
    for axis in (1, 2):
        for bit in (1, 2):
            blocks = [lax.slice_in_dim(t, i * b, (i + 1) * b, axis=axis) for i in range(4)]
            swapped = jnp.concatenate([blocks[i ^ bit] for i in range(4)], axis=axis)
            t = jnp.where((place & bit) != 0, swapped, t)
    return t


def line_form(eigvecs, y_panels, t_factors):
    place = lax.axis_index("pcol")
    row = lax.axis_index("prow")
    outer = (row == 0) | (row == 3)
    panels, rows, width = y_panels.shape
    cols = eigvecs.shape[1]
    step = cols // SPLIT

    own = jnp.transpose(y_panels, (0, 2, 1))
    with jax.named_scope("gather"):
        sib = lax.ppermute(own, "pcol", CORE)
        far = lax.ppermute(own, "pcol", ACROSS)
        far_sib = lax.ppermute(far, "pcol", CORE)
    slices = [own, sib, far, far_sib]

    parts = []
    for s in range(4):
        with jax.named_scope(f"P{s}"):
            part = mm(slices[s].reshape(panels * width, rows), eigvecs, 1, 0)
        for j in range(SPLIT):
            parts.append(part[:, j * step:(j + 1) * step])

    y0 = jnp.concatenate([s[0] for s in slices], axis=0)
    y1 = jnp.concatenate([s[1] for s in slices], axis=0)
    cross_part = mm(own[0], y1, 1, 1)
    with jax.named_scope("G"):
        got = lax.ppermute(cross_part, "prow", EDGE)
        half = cross_part + got
        mid = lax.ppermute(half, "prow", MIDDLE)
        both = half + mid
        back = lax.ppermute(both, "prow", EDGE)
        cross_own = jnp.where(outer, back, both)
        cross_sib = lax.ppermute(cross_own, "pcol", CORE)
        cross_far = lax.ppermute(cross_own, "pcol", ACROSS)
        cross_fs = lax.ppermute(cross_far, "pcol", CORE)
    stacked = []
    for s, block in enumerate((cross_own, cross_sib, cross_far, cross_fs)):
        order = [block[:, (i ^ s) * width:((i ^ s) + 1) * width] for i in range(4)]
        stacked.append(jnp.concatenate(order, axis=1))
    cross = jnp.concatenate(stacked, axis=0)

    tri = relative_blocks(t_factors, place)
    a0 = mm(tri[0], y0, 0, 0)
    a1 = mm(tri[1], y1 - mm(cross, a0, 0, 0), 0, 0)
    lhs = jnp.concatenate(
        [x[s * width:(s + 1) * width] for s in range(4) for x in (a0, a1)], axis=0
    )

    count = len(parts)
    edge, middle, summed = {}, {}, {}
    total = {}
    for t in range(count + LAG_E):
        back = t - LAG_E
        if back >= 0:
            summed[back] = summed[back] + middle[back]
        with jax.named_scope(f"Ein{t}"):
            if back < 0:
                sent = parts[t]
            elif t < count:
                sent = jnp.where(outer, parts[t], summed[back])
            else:
                sent = summed[back]
        with jax.named_scope(f"E{t}"):
            edge[t] = lax.ppermute(sent, "prow", EDGE)
        if back >= 0:
            total[back] = jnp.where(outer, edge[t], summed[back])
        c = t - LAG_M
        if 0 <= c < count:
            with jax.named_scope(f"Madd{c}"):
                summed[c] = parts[c] + edge[c]
            with jax.named_scope(f"M{c}"):
                middle[c] = lax.ppermute(summed[c], "prow", MIDDLE)

    blocks = []
    for j in range(SPLIT):
        rhs = jnp.concatenate([total[s * SPLIT + j] for s in range(4)], axis=0)
        with jax.named_scope(f"U{j}"):
            blocks.append(eigvecs[:, j * step:(j + 1) * step] - mm(lhs, rhs, 0, 0))
    return jnp.concatenate(blocks, axis=1)


def solution(mesh):
    line = mesh.shape["prow"] == 4 and mesh.shape["pcol"] == 4
    return jax.shard_map(
        line_form if line else ring_form,
        mesh=mesh,
        in_specs=(
            P(("grp", "prow"), "pcol"),
            P(None, ("grp", "prow"), "pcol"),
            P("grp", None, None),
        ),
        out_specs=P(("grp", "prow"), "pcol"),
        check_vma=False,
    )
```
